256 devices in a mesh: seq: 32 (over y, z_hi, core), width: 8 (over x, z_lo).
Axes of the slice: x: 4, y: 4, z: 8 (z_hi: 4, z_lo: 2; z = z_hi * 2 + z_lo), core: 2. Of those that a mesh axis runs over, the one named last changes fastest.
Arguments:
- tokens: bfloat16 [32768, 16384], P('seq', 'width'), may hold values from -6 to 6
- panel_weights: bfloat16 [2, 16384, 1024], P(None, 'width', 'seq'), may hold values from -0.046875 to 0.046875
- panel_scales: float32 [2, 1024, 1024], P(None, 'width', 'seq'), may hold values from 0.4 to 2.5
- doc_lengths: int32 [32, 8], P('seq'), may hold values from 0 to 1024, as said below
Outputs:
- hidden: float32 [32768, 1024], P(('seq', 'width'))
The draws below stay inside these ranges and needn't reach their ends.
Inputs may be any that keep to these rules, and one draw needn't show every extreme that they name: `doc_lengths`: each row sums to at most 1024; some row holds one document of exactly 1024; documents may be empty.
All inputs are finite; a program needn't handle non-finite values.
Results may differ from the reference program's by a relative error of at most 0.014.
Values may be sent and summed in bfloat16 or wider, within the bound.
No kernel may reach another device: no remote copies, remote signals or barrier semaphores. Data moves between devices by JAX's collectives and lax.ppermute only.
A program may use at most 64 MiB of HBM per device.

```python
import math
import jax
import jax.numpy as jnp

D = 16384
PANEL = 1024
DOCS = 8
TOK_DEV = 1024
TOKENS = 32768
N_SEQ = 32


def draw_doc_lengths(key, part):
    first, second, third = jax.random.split(jax.random.fold_in(key, 7), 3)
    filled = jax.random.randint(first, (N_SEQ,), TOK_DEV // 8, TOK_DEV // 2 + 1)
    busiest = jax.random.randint(second, (), 0, N_SEQ)
    filled = jnp.where(jnp.arange(N_SEQ) == busiest, TOK_DEV, filled).astype(jnp.int32)
    cut_points = jax.random.randint(third, (N_SEQ, DOCS - 1), 0, TOK_DEV + 1)
    cut_points = jnp.sort(jnp.minimum(cut_points, filled[:, None]), axis=1).astype(jnp.int32)
    edges = jnp.concatenate([jnp.zeros((N_SEQ, 1), jnp.int32), cut_points, filled[:, None]], axis=1)
    lengths = jnp.diff(edges, axis=1).astype(jnp.int32)
    single = jnp.where(jnp.arange(DOCS)[None, :] == 0, TOK_DEV, 0).astype(jnp.int32)
    return jnp.where(jnp.arange(N_SEQ)[:, None] == busiest, single, lengths).astype(jnp.int32)


def levels(stream_key, dims, cuts, smallest, top_value):
    gain, own = 1.0, jax.random.fold_in(stream_key, 6)
    for axis_at, parts in cuts:
        heights = jnp.exp(jax.random.uniform(jax.random.fold_in(own, axis_at), (parts,), jnp.float32, smallest / len(cuts), top_value / len(cuts)))
        gain = gain * jnp.repeat(heights, dims[axis_at] // parts).reshape([-1 if axis == axis_at else 1 for axis in range(len(dims))])
    return gain


def bell_draw(key, shape, deviation, limit, cuts=(), kind=jnp.bfloat16):
    gain = levels(key, shape, cuts, -0.22, 0.18) if cuts else 1.0
    entries = jax.random.normal(key, shape, jnp.float32) * deviation * gain
    return jnp.minimum(jnp.maximum(entries, -limit), limit).astype(kind)


def setup_inputs(seed: int = 0) -> dict:
    keys = jax.random.split(jax.random.key(seed), 5)
    tokens = bell_draw(keys[0], (TOKENS, D), 1.0, 6.0, ((0, 32), (1, 8)))
    panel_weights = bell_draw(keys[1], (2, D, PANEL), D ** -0.5, 0.046875, ((1, 8), (2, 32)))
    panel_scales = jnp.clip(jnp.exp(math.log(2.5) - 1.8325814 * jax.random.uniform(keys[2], (2, D // 16, PANEL), jnp.float32) ** levels(keys[2], (2, D // 16, PANEL), ((1, 8), (2, 32)), -0.2, 0.2)), 0.4, 2.5)
    doc_lengths = draw_doc_lengths(jax.random.fold_in(keys[4], 71), 0)
    return dict(tokens=tokens, panel_weights=panel_weights, panel_scales=panel_scales, doc_lengths=doc_lengths)


def dequantize(weights, scales):
    spread = jnp.repeat(scales, 16, axis=1)
    return (weights.astype(jnp.float32) * spread).astype(jnp.bfloat16)


def reference(tokens, panel_weights, panel_scales, doc_lengths):
    weights_deq = dequantize(panel_weights, panel_scales)
    gate = jnp.dot(tokens, weights_deq[0], preferred_element_type=jnp.float32)
    upward = jnp.dot(tokens, weights_deq[1], preferred_element_type=jnp.float32)
    mixed = jax.nn.silu(gate) * upward
    live_count = jnp.sum(doc_lengths, axis=1).astype(jnp.int32)
    index_all = jnp.arange(TOKENS, dtype=jnp.int32)
    owner = index_all // TOK_DEV
    position = index_all % TOK_DEV
    keep = position < live_count[owner]
    return jnp.where(keep[:, None], mixed, jnp.float32(0.0)).astype(jnp.float32)
```

```python
import functools

import jax
import jax.numpy as jnp
from jax import lax
from jax.experimental import pallas as pl
from jax.experimental.pallas import tpu as pltpu
from jax.sharding import PartitionSpec as P

NY, NZ, NX = 4, 4, 4
ORDER = (2, 1, 3, 0)
NT = (((1,), (1,)), ((), ()))


def seq_shift(v, dy=0, dz=0, flip=0):
    pairs = []
    for y in range(NY):
        for z in range(NZ):
            for c in range(2):
                to = (((y + dy) % NY) * NZ + (z + dz) % NZ) * 2 + (c ^ flip)
                pairs.append(((y * NZ + z) * 2 + c, to))
    return lax.ppermute(v, "seq", pairs)


def width_shift(v, dx, dl):
    pairs = []
    for x in range(NX):
        for l in range(2):
            pairs.append((x * 2 + l, ((x + dx) % NX) * 2 + (l ^ dl)))
    return lax.ppermute(v, "width", pairs)


def dequant_kernel(w_ref, s_ref, o_ref):
    groups = s_ref.shape[1]
    depth = w_ref.shape[1]
    row = lax.broadcasted_iota(jnp.int32, (groups, depth), 0)
    col = lax.broadcasted_iota(jnp.int32, (groups, depth), 1)
    pick = jnp.where(col // 16 == row, 1.0, 0.0).astype(jnp.float32)
    spread = jnp.dot(
        s_ref[...], pick, precision=lax.Precision.HIGHEST,
        preferred_element_type=jnp.float32,
    )
    o_ref[...] = (w_ref[...].astype(jnp.float32) * spread).astype(jnp.bfloat16)


def dequant(w, s):
    return pl.pallas_call(
        dequant_kernel,
        out_shape=jax.ShapeDtypeStruct(w.shape, jnp.bfloat16),
    )(w, s)


def matmul_kernel(nb, place, ta_ref, tb_ref, *refs):
    shards, outs = refs[: 3 * nb], refs[3 * nb : 3 * nb + 8]
    w_ref, pa_ref, pb_ref = refs[3 * nb + 8 :]
    step = pl.program_id(0)

    @pl.when(step == 0)
    def _():
        for b in range(nb):
            own, side, far = shards[3 * b : 3 * b + 3]
            for half in range(2):
                base = b * 256 + half * 128
                lo = half * 32
                w_ref[base : base + 32] = own[lo : lo + 32]
                w_ref[base + 32 : base + 64] = side[64 + lo : 96 + lo]
                w_ref[base + 64 : base + 96] = far[lo : lo + 32]
                w_ref[base + 96 : base + 128] = side[lo : lo + 32]

    for t_ref, p_ref in ((ta_ref, pa_ref), (tb_ref, pb_ref)):
        p_ref[...] = lax.dot_general(
            t_ref[...], w_ref[...], NT, preferred_element_type=jnp.float32
        ).astype(jnp.bfloat16)
    here = place[0]
    for i, dx in enumerate(ORDER):

        @pl.when(step == i)
        def _(dx=dx):
            for dl in range(2):
                rows = pl.ds(pl.multiple_of((here ^ dl) * 128, 128), 128)
                outs[dx * 2 + dl][0:128] = pa_ref[rows]
                outs[dx * 2 + dl][128:256] = pb_ref[rows]


def matmul(place, ta, tb, blocks):
    nb = len(blocks)
    shards = [s for block in blocks for s in block]
    n = nb * 256
    depth = ta.shape[1]
    whole = lambda a: pl.BlockSpec(a.shape, lambda i, p: (0, 0))
    tok = pl.BlockSpec((256, depth), lambda i, p: (p[1 + i], 0))
    return pl.pallas_call(
        functools.partial(matmul_kernel, nb),
        out_shape=[jax.ShapeDtypeStruct((256, n), jnp.bfloat16)] * 8,
        grid_spec=pltpu.PrefetchScalarGridSpec(
            num_scalar_prefetch=1,
            grid=(4,),
            in_specs=[tok, tok] + [whole(s) for s in shards],
            out_specs=[pl.BlockSpec((256, n), lambda i, p: (0, 0))] * 8,
            scratch_shapes=[
                pltpu.VMEM((n, depth), jnp.bfloat16),
                pltpu.VMEM((256, n), jnp.bfloat16),
                pltpu.VMEM((256, n), jnp.bfloat16),
            ],
        ),
        compiler_params=pltpu.CompilerParams(dimension_semantics=("arbitrary",)),
        cost_estimate=pl.CostEstimate(
            flops=2 * 2048 * n * depth,
            bytes_accessed=2 * (2048 * depth + n * depth + 2048 * n),
            transcendentals=0,
        ),
    )(place, ta, tb, *shards)


def gated_kernel(nb, *refs):
    parts, (mine_ref, other_ref) = refs[:8], refs[8:]
    for b in range(nb):
        for rows, o_ref in ((0, mine_ref), (128, other_ref)):
            sums = []
            for half in range(2):
                col = b * 256 + half * 128
                terms = [p[rows : rows + 128, col : col + 128].astype(jnp.float32) for p in parts]
                while len(terms) > 1:
                    terms = [a + c for a, c in zip(terms[::2], terms[1::2])]
                sums.append(terms[0])
            gate, up = sums
            o_ref[:, b * 128 : b * 128 + 128] = gate / (1.0 + jnp.exp(-gate)) * up


def gated(parts):
    nb = parts[0].shape[1] // 256
    half = jax.ShapeDtypeStruct((128, nb * 128), jnp.float32)
    return pl.pallas_call(
        functools.partial(gated_kernel, nb), out_shape=[half, half]
    )(*parts)


def finish_kernel(place, *refs):
    mine, theirs, o_ref = refs[:3], refs[3:6], refs[6]
    core, zh, y, live = place[0], place[1], place[2], place[3]
    rows = lax.broadcasted_iota(jnp.int32, (128, 128), 0)
    seg = lax.broadcasted_iota(jnp.int32, (128, 128), 1) // 32
    keep = rows < live
    first = jnp.full((128, 128), core, jnp.int32) == 0
    for rel, (which, b) in {0: (0, 0), 1: (1, 1), 3: (1, 0), 2: (2, 0)}.items():
        m = mine[which][:, b * 128 : b * 128 + 128]
        t = theirs[which][:, b * 128 : b * 128 + 128]
        m = jnp.where(keep, m, 0.0)
        t = jnp.where(keep, t, 0.0)
        even = pltpu.roll(jnp.where(first, m, t), zh * 32, 1)
        odd = pltpu.roll(jnp.where(first, t, m), zh * 32, 1)
        r = lambda v, s: pltpu.roll(v, s, 1)
        e32, o32 = r(even, 32), r(odd, 32)
        lo = jnp.where(seg == 0, even, jnp.where(seg == 1, o32, jnp.where(seg == 2, e32, r(odd, 64))))
        e96, o96 = r(even, 96), r(odd, 96)
        hi = jnp.where(seg == 0, r(even, 64), jnp.where(seg == 1, o96, jnp.where(seg == 2, e96, odd)))
        block = lax.rem(y + rel, NY) * 256
        o_ref[:, pl.ds(pl.multiple_of(block, 128), 128)] = lo
        o_ref[:, pl.ds(pl.multiple_of(block + 128, 128), 128)] = hi


def finish(place, mine, theirs):
    vm = pl.BlockSpec(memory_space=pltpu.VMEM)
    return pl.pallas_call(
        finish_kernel,
        out_shape=jax.ShapeDtypeStruct((128, 1024), jnp.float32),
        in_specs=[pl.BlockSpec(memory_space=pltpu.SMEM)] + [vm] * 6,
        out_specs=vm,
    )(place, *mine, *theirs)


def per_device(tokens, panel_weights, panel_scales, doc_lengths):
    seq, width = lax.axis_index("seq"), lax.axis_index("width")
    core, zh, y = seq % 2, (seq // 2) % NZ, seq // (2 * NZ)
    x, zl = width // 2, width % 2
    live = jnp.sum(doc_lengths) - width * 128

    partner = seq_shift(tokens, flip=1)
    w = jnp.transpose(panel_weights, (0, 2, 1)).reshape(64, -1)
    s = jnp.transpose(panel_scales, (0, 2, 1)).reshape(64, -1)
    own = dequant(w, s)

    below = seq_shift(own, dz=1)
    above = seq_shift(own, dz=-1)
    own_p, own_m = seq_shift(own, dy=-1), seq_shift(own, dy=1)
    far_g = seq_shift(below[:32], dz=1)
    far_u = seq_shift(above[32:], dz=-1)
    side = jnp.concatenate([below, above], 0)
    far = jnp.concatenate([far_g, far_u], 0)
    side_p, side_m = seq_shift(side, dy=-1), seq_shift(side, dy=1)
    far_p, far_m = seq_shift(far, dy=-1), seq_shift(far, dy=1)
    own_o = seq_shift(own_p, dy=-1)
    side_o = seq_shift(side_m, dy=1)
    far_o = seq_shift(far_p, dy=-1)

    place = jnp.stack([zl] + [(x + dx) % NX for dx in ORDER]).astype(jnp.int32)
    groups = [
        [(own, side, far)],
        [(own_m, side_m, far_m), (own_p, side_p, far_p)],
        [(own_o, side_o, far_o)],
    ]
    mine, theirs = [], []
    for blocks in groups:
        outs = matmul(place, tokens, partner, blocks)
        parts = [outs[0]]
        for dx, dl in ((2, 1), (2, 0), (1, 1), (3, 1), (1, 0), (3, 0), (0, 1)):
            parts.append(width_shift(outs[dx * 2 + dl], dx, dl))
        a, b = gated(parts)
        mine.append(a)
        theirs.append(seq_shift(b, flip=1))
    at = jnp.stack([core, zh, y, live]).astype(jnp.int32)
    return finish(at, mine, theirs)


def solution(mesh):
    in_specs = (P("seq", "width"), P(None, "width", "seq"), P(None, "width", "seq"), P("seq", None))
    out_specs = P(("seq", "width"), None)
    return jax.shard_map(
        per_device, mesh=mesh, in_specs=in_specs, out_specs=out_specs, check_vma=False
    )
```

```python
import functools

import jax
import jax.numpy as jnp
from jax import lax
from jax.experimental import pallas as pl
from jax.experimental.pallas import tpu as pltpu
from jax.sharding import PartitionSpec as P

NY, NZ, NX = 4, 4, 4
ORDER = (2, 1, 3, 0)
NT = (((1,), (1,)), ((), ()))
GROUPS = (
    (((0, 0), (1, 0), (3, 0), (2, 0)),),
    (((1, 1), (1, 3), (3, 1), (3, 3)), ((0, 1), (0, 3), (0, 2), (1, 2))),
    (((3, 2), (2, 1), (2, 3), (2, 2)),),
)
WHERE = {s: (g, t, i) for g, tiles in enumerate(GROUPS) for t, tile in enumerate(tiles) for i, s in enumerate(tile)}

VM = pl.BlockSpec(memory_space=pltpu.VMEM)
SM = pl.BlockSpec(memory_space=pltpu.SMEM)


def limit(mib):
    return pltpu.CompilerParams(vmem_limit_bytes=mib << 20)


def seq_shift(v, dy=0, dz=0, flip=0):
    pairs = []
    for y in range(NY):
        for z in range(NZ):
            for c in range(2):
                to = (((y + dy) % NY) * NZ + (z + dz) % NZ) * 2 + (c ^ flip)
                pairs.append(((y * NZ + z) * 2 + c, to))
    return lax.ppermute(v, "seq", pairs)


def width_shift(v, dx, dl):
    pairs = []
    for x in range(NX):
        for l in range(2):
            pairs.append((x * 2 + l, ((x + dx) % NX) * 2 + (l ^ dl)))
    return lax.ppermute(v, "width", pairs)


def dequant_kernel(w_ref, s_ref, o_ref):
    groups = s_ref.shape[1]
    depth = w_ref.shape[1]
    row = lax.broadcasted_iota(jnp.int32, (groups, depth), 0)
    col = lax.broadcasted_iota(jnp.int32, (groups, depth), 1)
    pick = jnp.where(col // 16 == row, 1.0, 0.0).astype(jnp.float32)
    spread = jnp.dot(
        s_ref[...], pick, precision=lax.Precision.HIGHEST,
        preferred_element_type=jnp.float32,
    )
    o_ref[...] = (w_ref[...].astype(jnp.float32) * spread).astype(jnp.bfloat16)


def dequant(w, s):
    return pl.pallas_call(
        dequant_kernel,
        out_shape=jax.ShapeDtypeStruct(w.shape, jnp.bfloat16),
        in_specs=[VM, VM],
        out_specs=VM,
        compiler_params=limit(8),
    )(w, s)


def matmul_kernel(pieces, count, place, ta_ref, tb_ref, *refs):
    shards, outs = refs[:count], refs[count:-2]
    w_ref, p_ref = refs[-2:]
    for at, (which, row) in enumerate(pieces):
        w_ref[at * 32 : at * 32 + 32] = shards[which][row : row + 32]
    here = place[0]

    def quarter(i, _):
        rows = pl.ds(pl.multiple_of(place[1 + i] * 256, 256), 256)
        for k, t_ref in enumerate((ta_ref, tb_ref)):
            part = lax.dot_general(
                t_ref[rows], w_ref[...], NT, preferred_element_type=jnp.float32
            ).astype(jnp.bfloat16)
            for l in range(2):
                to = (here ^ l) * 256 + k * 128
                p_ref[i, pl.ds(pl.multiple_of(to, 128), 128)] = part[l * 128 : l * 128 + 128]
        return 0

    lax.fori_loop(0, 4, quarter, 0)
    split = len(outs) // 4
    size = 512 // split
    for i, dx in enumerate(ORDER):
        for j in range(split):
            outs[dx * split + j][...] = p_ref[i, j * size : j * size + size]


def matmul(place, ta, tb, tiles, arrays, split):
    names, pieces = [], []
    for tile in tiles:
        for half in range(2):
            for name, row in tile:
                if name not in names:
                    names.append(name)
                pieces.append((names.index(name), row + half * 32))
    n, depth = len(tiles) * 256, ta.shape[1]
    return pl.pallas_call(
        functools.partial(matmul_kernel, pieces, len(names)),
        out_shape=[jax.ShapeDtypeStruct((512 // split, n), jnp.bfloat16)] * (4 * split),
        in_specs=[SM] + [VM] * (2 + len(names)),
        out_specs=[VM] * (4 * split),
        scratch_shapes=[
            pltpu.VMEM((n, depth), jnp.bfloat16),
            pltpu.VMEM((4, 512, n), jnp.bfloat16),
        ],
        compiler_params=limit(24),
        cost_estimate=pl.CostEstimate(
            flops=2 * 2048 * n * depth,
            bytes_accessed=2 * (2048 * depth + n * depth + 2048 * n),
            transcendentals=0,
        ),
    )(place, ta, tb, *[arrays[k] for k in names])


def combine_kernel(a_ref, b_ref, c_ref, d_ref, keep_ref, send_ref):
    f = lambda r, s: r[s].astype(jnp.float32)
    lo, hi = slice(0, 256), slice(256, 512)
    keep_ref[...] = (f(a_ref, lo) + f(b_ref, lo)) + (f(c_ref, lo) + f(d_ref, lo))
    send_ref[...] = ((f(a_ref, hi) + f(b_ref, hi)) + (f(c_ref, hi) + f(d_ref, hi))).astype(jnp.bfloat16)


def combine(parts):
    n = parts[0].shape[1]
    return pl.pallas_call(
        combine_kernel,
        out_shape=[jax.ShapeDtypeStruct((256, n), jnp.float32), jax.ShapeDtypeStruct((256, n), jnp.bfloat16)],
        in_specs=[VM] * 4,
        out_specs=[VM] * 2,
        compiler_params=limit(8),
    )(*parts)


def gated_kernel(nb, *refs):
    parts, (mine_ref, other_ref) = refs[:-2], refs[-2:]
    for b in range(nb):
        for rows, o_ref in ((0, mine_ref), (128, other_ref)):
            sums = []
            for half in range(2):
                col = b * 256 + half * 128
                terms = [p[rows : rows + 128, col : col + 128].astype(jnp.float32) for p in parts]
                while len(terms) > 1:
                    terms = [a + c for a, c in zip(terms[::2], terms[1::2])]
                sums.append(terms[0])
            gate, up = sums
            o_ref[:, b * 128 : b * 128 + 128] = gate / (1.0 + jnp.exp(-gate)) * up


def gated(parts):
    nb = parts[0].shape[1] // 256
    half = jax.ShapeDtypeStruct((128, nb * 128), jnp.float32)
    return pl.pallas_call(
        functools.partial(gated_kernel, nb),
        out_shape=[half, half],
        in_specs=[VM] * len(parts),
        out_specs=[VM] * 2,
        compiler_params=limit(8),
    )(*parts)


def finish_kernel(place, *refs):
    mine, theirs, o_ref = refs[:3], refs[3:6], refs[6]
    core, zh, y, live = place[0], place[1], place[2], place[3]
    rows = lax.broadcasted_iota(jnp.int32, (128, 128), 0)
    seg = lax.broadcasted_iota(jnp.int32, (128, 128), 1) // 32
    keep = rows < live
    first = jnp.full((128, 128), core, jnp.int32) == 0
    turn = lambda v, s: pltpu.roll(v, s % 128, 1) if s % 128 else v

    def ordered(side, ry):
        whole = None
        for rz in range(NZ):
            g, t, i = WHERE[(ry, rz)]
            piece = turn(side[g][:, t * 128 : t * 128 + 128], 32 * (rz - i))
            whole = piece if whole is None else jnp.where(seg == rz, piece, whole)
        return pltpu.roll(jnp.where(keep, whole, 0.0), zh * 32, 1)

    for ry in range(NY):
        m, t = ordered(mine, ry), ordered(theirs, ry)
        even, odd = jnp.where(first, m, t), jnp.where(first, t, m)
        lo = jnp.where(seg < 2, jnp.where(seg == 0, even, turn(odd, 32)), jnp.where(seg == 2, turn(even, 32), turn(odd, 64)))
        hi = jnp.where(seg < 2, jnp.where(seg == 0, turn(even, 64), turn(odd, 96)), jnp.where(seg == 2, turn(even, 96), odd))
        block = lax.rem(y + ry, NY) * 256
        o_ref[:, pl.ds(pl.multiple_of(block, 128), 128)] = lo
        o_ref[:, pl.ds(pl.multiple_of(block + 128, 128), 128)] = hi


def finish(place, mine, theirs):
    return pl.pallas_call(
        finish_kernel,
        out_shape=jax.ShapeDtypeStruct((128, 1024), jnp.float32),
        in_specs=[SM] + [VM] * 6,
        out_specs=VM,
        compiler_params=limit(8),
    )(place, *mine, *theirs)


def per_device(tokens, panel_weights, panel_scales, doc_lengths):
    seq, width = lax.axis_index("seq"), lax.axis_index("width")
    core, zh, y = seq & 1, (seq >> 1) & 3, seq >> 3
    x, zl = width >> 1, width & 1
    live = jnp.sum(doc_lengths) - width * 128

    partner = seq_shift(tokens, flip=1)
    w = jnp.transpose(panel_weights, (0, 2, 1)).reshape(64, -1)
    s = jnp.transpose(panel_scales, (0, 2, 1)).reshape(64, -1)
    own = dequant(w, s)

    below, above = seq_shift(own, dz=1), seq_shift(own, dz=-1)
    own_p, own_m, own_o = seq_shift(own, dy=-1), seq_shift(own, dy=1), seq_shift(own, dy=2)
    far = seq_shift(own, dz=2)
    side = jnp.concatenate([below, above], 0)
    side_p, side_m = seq_shift(side, dy=-1), seq_shift(side, dy=1)
    below_o, above_o = seq_shift(side_m[:64], dy=1), seq_shift(side_p[64:], dy=-1)
    far_p, far_m, far_o = seq_shift(far, dy=-1), seq_shift(far, dy=1), seq_shift(far, dy=2)

    arrays = dict(
        own=own, own_p=own_p, own_m=own_m, own_o=own_o,
        side=side, side_p=side_p, side_m=side_m, below_o=below_o, above_o=above_o,
        far=far, far_p=far_p, far_m=far_m, far_o=far_o,
    )
    tag = {0: "", 1: "_p", 3: "_m", 2: "_o"}

    def shard(ry, rz):
        if rz == 0:
            return "own" + tag[ry], 0
        if rz == 2:
            return "far" + tag[ry], 0
        if ry == 2:
            return ("above_o" if rz == 1 else "below_o"), 0
        return "side" + tag[ry], (64 if rz == 1 else 0)

    place = jnp.stack([zl] + [(x + dx) & 3 for dx in ORDER]).astype(jnp.int32)
    at = jnp.stack([core, zh, y, live]).astype(jnp.int32)
    mine, theirs = [], []
    for g, tiles in enumerate(GROUPS):
        named = [[shard(*s) for s in tile] for tile in tiles]
        if g < 2:
            outs = matmul(place, tokens, partner, named, arrays, 1)
            got = [width_shift(outs[dx], dx, 0) for dx in (2, 1, 3)]
            keep, send = combine([outs[0]] + got)
            a, b = gated([keep, width_shift(send, 0, 1)])
        else:
            outs = matmul(place, tokens, partner, named, arrays, 2)
            parts = [outs[0]]
            for dx, dl in ((2, 1), (2, 0), (1, 1), (3, 1), (1, 0), (3, 0), (0, 1)):
                parts.append(width_shift(outs[dx * 2 + dl], dx, dl))
            a, b = gated(parts)
        mine.append(a)
        theirs.append(seq_shift(b, flip=1))
    return finish(at, mine, theirs)


def solution(mesh):
    in_specs = (P("seq", "width"), P(None, "width", "seq"), P(None, "width", "seq"), P("seq", None))
    out_specs = P(("seq", "width"), None)
    return jax.shard_map(
        per_device, mesh=mesh, in_specs=in_specs, out_specs=out_specs, check_vma=False
    )
```

```python
import functools

import jax
import jax.numpy as jnp
from jax import lax
from jax.experimental import pallas as pl
from jax.experimental.pallas import tpu as pltpu
from jax.sharding import PartitionSpec as P


NY, NZ, NX = 4, 4, 4
ORDER = (2, 1, 3, 0)
NT = (((1,), (1,)), ((), ()))
GROUPS = (
    (((0, 0), (1, 0), (3, 0), (2, 0)), ((0, 1), (0, 3))),
    (((1, 1), (1, 3), (3, 1), (3, 3)),),
    (((0, 2), (1, 2), (3, 2), (2, 2)), ((2, 1), (2, 3))),
)
WHERE = {s: (g, t, i) for g, tiles in enumerate(GROUPS) for t, tile in enumerate(tiles) for i, s in enumerate(tile)}


VM = pl.BlockSpec(memory_space=pltpu.VMEM)
SM = pl.BlockSpec(memory_space=pltpu.SMEM)


def limit(mib):
    return pltpu.CompilerParams(vmem_limit_bytes=mib << 20)


def seq_shift(v, dy=0, dz=0, flip=0):
    pairs = []
    for y in range(NY):
        for z in range(NZ):
            for c in range(2):
                to = (((y + dy) % NY) * NZ + (z + dz) % NZ) * 2 + (c ^ flip)
                pairs.append(((y * NZ + z) * 2 + c, to))
    return lax.ppermute(v, "seq", pairs)


def width_shift(v, dx, dl):
    pairs = []
    for x in range(NX):
        for l in range(2):
            pairs.append((x * 2 + l, ((x + dx) % NX) * 2 + (l ^ dl)))
    return lax.ppermute(v, "width", pairs)


def dequant_kernel(w_ref, s_ref, o_ref):
    groups = s_ref.shape[1]
    depth = w_ref.shape[1]
    row = lax.broadcasted_iota(jnp.int32, (groups, depth), 0)
    col = lax.broadcasted_iota(jnp.int32, (groups, depth), 1)
    pick = jnp.where(col // 16 == row, 1.0, 0.0).astype(jnp.float32)
    spread = jnp.dot(
        s_ref[...], pick, precision=lax.Precision.HIGHEST,
        preferred_element_type=jnp.float32,
    )
    o_ref[...] = (w_ref[...].astype(jnp.float32) * spread).astype(jnp.bfloat16)


def dequant(w, s):
    return pl.pallas_call(
        dequant_kernel,
        out_shape=jax.ShapeDtypeStruct(w.shape, jnp.bfloat16),
        in_specs=[VM, VM],
        out_specs=VM,
        compiler_params=limit(8),
    )(w, s)


def load_kernel(place, a_ref, b_ref, o_ref):
    o_ref[...] = a_ref[0:8, 0:128] + b_ref[0:8, 0:128]


def load(place, a, b):
    return pl.pallas_call(
        load_kernel,
        out_shape=jax.ShapeDtypeStruct((8, 128), a.dtype),
        in_specs=[SM] + [VM] * 2,
        out_specs=VM,
        compiler_params=limit(16),
    )(place, a, b)


def matmul_kernel(pieces, count, place, ta_ref, tb_ref, *refs):
    shards, outs = refs[:count], refs[count + 1 : -2]
    w_ref, p_ref = refs[-2:]
    for at, (which, row) in enumerate(pieces):
        w_ref[at * 32 : at * 32 + 32] = shards[which][row : row + 32]
    here = place[0]

    def half(h, _):
        rows = pl.ds(pl.multiple_of(h * 512, 512), 512)
        for k, t_ref in enumerate((ta_ref, tb_ref)):
            p_ref[k, rows] = lax.dot_general(
                t_ref[rows], w_ref[...], NT, preferred_element_type=jnp.float32
            ).astype(jnp.bfloat16)
        return 0

    lax.fori_loop(0, 2, half, 0)
    split = len(outs) // 4
    for i, dx in enumerate(ORDER):
        for l in range(2):
            row = pl.multiple_of(place[1 + i] * 256 + (here ^ l) * 128, 128)
            for k in range(2):
                out = outs[dx * split + l * (split - 1)]
                to = l * 256 * (2 - split) + k * 128
                out[to : to + 128] = p_ref[k, pl.ds(row, 128)]


def matmul(place, ta, tb, tiles, arrays, ready, split):
    names, pieces = [], []
    for tile in tiles:
        for half in range(2):
            for name, row in tile:
                if name not in names:
                    names.append(name)
                pieces.append((names.index(name), row + half * 32))
    n, depth = 32 * len(pieces), ta.shape[1]
    return pl.pallas_call(
        functools.partial(matmul_kernel, pieces, len(names)),
        out_shape=[jax.ShapeDtypeStruct((512 // split, n), jnp.bfloat16)] * (4 * split),
        in_specs=[SM] + [VM] * (3 + len(names)),
        out_specs=[VM] * (4 * split),
        scratch_shapes=[
            pltpu.VMEM((n, depth), jnp.bfloat16),
            pltpu.VMEM((2, 1024, n), jnp.bfloat16),
        ],
        compiler_params=limit(24),
        cost_estimate=pl.CostEstimate(
            flops=2 * 2048 * n * depth,
            bytes_accessed=2 * (2048 * depth + n * depth + 2048 * n),
            transcendentals=0,
        ),
    )(place, ta, tb, *[arrays[k] for k in names], ready)


def combine_kernel(a_ref, b_ref, c_ref, d_ref, keep_ref, send_ref):
    f = lambda r, s: r[s].astype(jnp.float32)
    lo, hi = slice(0, 256), slice(256, 512)
    keep_ref[...] = (f(a_ref, lo) + f(b_ref, lo)) + (f(c_ref, lo) + f(d_ref, lo))
    send_ref[...] = ((f(a_ref, hi) + f(b_ref, hi)) + (f(c_ref, hi) + f(d_ref, hi))).astype(jnp.bfloat16)


def combine(parts):
    n = parts[0].shape[1]
    return pl.pallas_call(
        combine_kernel,
        out_shape=[jax.ShapeDtypeStruct((256, n), jnp.float32), jax.ShapeDtypeStruct((256, n), jnp.bfloat16)],
        in_specs=[VM] * 4,
        out_specs=[VM] * 2,
        compiler_params=limit(8),
    )(*parts)


def gated_kernel(sizes, *refs):
    parts, (mine_ref, other_ref) = refs[:-2], refs[-2:]
    for rows, o_ref in ((0, mine_ref), (128, other_ref)):

        def total(col):
            terms = [p[rows : rows + 128, col : col + 128].astype(jnp.float32) for p in parts]
            while len(terms) > 1:
                terms = [a + c for a, c in zip(terms[::2], terms[1::2])]
            return terms[0]

        col = 0
        for b, size in enumerate(sizes):
            gate = total(col)
            up = total(col + 128) if size == 4 else pltpu.roll(gate, 64, 1)
            col += 64 * size
            o_ref[:, b * 128 : b * 128 + 128] = gate / (1.0 + jnp.exp(-gate)) * up


def gated(parts, tiles):
    sizes = [len(tile) for tile in tiles]
    half = jax.ShapeDtypeStruct((128, len(sizes) * 128), jnp.float32)
    return pl.pallas_call(
        functools.partial(gated_kernel, sizes),
        out_shape=[half, half],
        in_specs=[VM] * len(parts),
        out_specs=[VM] * 2,
        compiler_params=limit(8),
    )(*parts)


def finish_kernel(place, docs, *refs):
    mine, theirs, o_ref = refs[:3], refs[3:6], refs[6]
    core, zh, y = place[5], place[6], place[7]
    live = -place[8]
    for i in range(docs.shape[1]):
        live += docs[0, i]
    rows = lax.broadcasted_iota(jnp.int32, (128, 128), 0)
    seg = lax.broadcasted_iota(jnp.int32, (128, 128), 1) // 32
    keep = rows < live
    first = jnp.full((128, 128), core, jnp.int32) == 0
    turn = lambda v, s: pltpu.roll(v, s % 128, 1) if s % 128 else v

    def ordered(side, ry):
        whole = None
        for rz in range(NZ):
            g, t, i = WHERE[(ry, rz)]
            piece = turn(side[g][:, t * 128 : t * 128 + 128], 32 * (rz - i))
            whole = piece if whole is None else jnp.where(seg == rz, piece, whole)
        return pltpu.roll(jnp.where(keep, whole, 0.0), zh * 32, 1)

    for ry in range(NY):
        m, t = ordered(mine, ry), ordered(theirs, ry)
        even, odd = jnp.where(first, m, t), jnp.where(first, t, m)
        lo = jnp.where(seg < 2, jnp.where(seg == 0, even, turn(odd, 32)), jnp.where(seg == 2, turn(even, 32), turn(odd, 64)))
        hi = jnp.where(seg < 2, jnp.where(seg == 0, turn(even, 64), turn(odd, 96)), jnp.where(seg == 2, turn(even, 96), odd))
        block = lax.rem(y + ry, NY) * 256
        o_ref[:, pl.ds(pl.multiple_of(block, 128), 128)] = lo
        o_ref[:, pl.ds(pl.multiple_of(block + 128, 128), 128)] = hi


def finish(place, docs, mine, theirs):
    return pl.pallas_call(
        finish_kernel,
        out_shape=jax.ShapeDtypeStruct((128, 1024), jnp.float32),
        in_specs=[SM] * 2 + [VM] * 6,
        out_specs=VM,
        compiler_params=limit(8),
    )(place, docs, *mine, *theirs)


def per_device(tokens, panel_weights, panel_scales, doc_lengths):
    seq, width = lax.axis_index("seq"), lax.axis_index("width")
    core, zh, y = seq & 1, (seq >> 1) & 3, seq >> 3
    x, zl = width >> 1, width & 1

    place = jnp.stack(
        [zl] + [(x + dx) & 3 for dx in ORDER] + [core, zh, y, width * 128]
    ).astype(jnp.int32)
    partner = seq_shift(tokens, flip=1)
    w = jnp.transpose(panel_weights, (0, 2, 1)).reshape(64, -1)
    s = jnp.transpose(panel_scales, (0, 2, 1)).reshape(64, -1)
    own = dequant(w, s)

    below, above = seq_shift(own, dz=1), seq_shift(own, dz=-1)
    own_p, own_m = seq_shift(own, dy=-1), seq_shift(own, dy=1)
    own_o = seq_shift(own, dy=2)
    ready = load(place, tokens, partner)
    far = seq_shift(own, dz=2)
    side = jnp.concatenate([below, above], 0)
    side_p, side_m = seq_shift(side, dy=-1), seq_shift(side, dy=1)
    below_o = seq_shift(side_m[:64], dy=1)
    above_o = seq_shift(side_p[64:], dy=-1)
    far_p, far_m = seq_shift(far, dy=-1), seq_shift(far, dy=1)
    far_o = seq_shift(far, dy=2)

    arrays = dict(
        own=own, own_p=own_p, own_m=own_m, own_o=own_o,
        side=side, side_p=side_p, side_m=side_m, below_o=below_o, above_o=above_o,
        far=far, far_p=far_p, far_m=far_m, far_o=far_o,
    )
    tag = {0: "", 1: "_p", 3: "_m", 2: "_o"}

    def shard(ry, rz):
        if rz == 0:
            return "own" + tag[ry], 0
        if rz == 2:
            return "far" + tag[ry], 0
        if ry == 2:
            return ("above_o" if rz == 1 else "below_o"), 0
        return "side" + tag[ry], (64 if rz == 1 else 0)

    mine, theirs = [], []
    for g, tiles in enumerate(GROUPS):
        named = [[shard(*s) for s in tile] for tile in tiles]
        outs = matmul(place, tokens, partner, named, arrays, ready, 1 if g < 2 else 2)
        if g < 2:
            got = [width_shift(outs[dx], dx, 0) for dx in (2, 1, 3)]
            keep, send = combine([outs[0]] + got)
            parts = [keep, width_shift(send, 0, 1)]
        else:
            parts = [outs[0]]
            for dx, dl in ((2, 1), (2, 0), (1, 1), (3, 1), (1, 0), (3, 0), (0, 1)):
                parts.append(width_shift(outs[dx * 2 + dl], dx, dl))
        a, b = gated(parts, tiles)
        mine.append(a)
        theirs.append(seq_shift(b, flip=1))
    return finish(place, doc_lengths, mine, theirs)


def solution(mesh):
    in_specs = (P("seq", "width"), P(None, "width", "seq"), P(None, "width", "seq"), P("seq", None))
    out_specs = P(("seq", "width"), None)
    return jax.shard_map(
        per_device, mesh=mesh, in_specs=in_specs, out_specs=out_specs, check_vma=False
    )
```

```python
import functools

import jax
import jax.numpy as jnp
from jax import lax
from jax.experimental import pallas as pl
from jax.experimental.pallas import tpu as pltpu
from jax.sharding import PartitionSpec as P


NY, NZ, NX = 4, 4, 4
ORDER = (2, 1, 3, 0)
NT = (((1,), (1,)), ((), ()))
GROUPS = (
    (((0, 0), (1, 0), (3, 0), (2, 0)), ((0, 1), (0, 3))),
    (((1, 1), (1, 3), (3, 1), (3, 3)),),
    (((0, 2), (1, 2), (3, 2), (2, 2)), ((2, 1), (2, 3))),
)
WHERE = {s: (g, t, i) for g, tiles in enumerate(GROUPS) for t, tile in enumerate(tiles) for i, s in enumerate(tile)}


VM = pl.BlockSpec(memory_space=pltpu.VMEM)
SM = pl.BlockSpec(memory_space=pltpu.SMEM)


def limit(mib):
    return pltpu.CompilerParams(vmem_limit_bytes=mib << 20)


def seq_shift(v, dy=0, dz=0, flip=0):
    pairs = []
    for y in range(NY):
        for z in range(NZ):
            for c in range(2):
                to = (((y + dy) % NY) * NZ + (z + dz) % NZ) * 2 + (c ^ flip)
                pairs.append(((y * NZ + z) * 2 + c, to))
    return lax.ppermute(v, "seq", pairs)


def width_shift(v, dx, dl):
    pairs = []
    for x in range(NX):
        for l in range(2):
            pairs.append((x * 2 + l, ((x + dx) % NX) * 2 + (l ^ dl)))
    return lax.ppermute(v, "width", pairs)


def dequant_kernel(w_ref, s_ref, o_ref):
    groups = s_ref.shape[1]
    depth = w_ref.shape[1]
    row = lax.broadcasted_iota(jnp.int32, (groups, depth), 0)
    col = lax.broadcasted_iota(jnp.int32, (groups, depth), 1)
    pick = jnp.where(col // 16 == row, 1.0, 0.0).astype(jnp.float32)
    spread = jnp.dot(
        s_ref[...], pick, precision=lax.Precision.HIGHEST,
        preferred_element_type=jnp.float32,
    )
    o_ref[...] = (w_ref[...].astype(jnp.float32) * spread).astype(jnp.bfloat16)


def dequant(w, s):
    return pl.pallas_call(
        dequant_kernel,
        out_shape=jax.ShapeDtypeStruct(w.shape, jnp.bfloat16),
        in_specs=[VM, VM],
        out_specs=VM,
        compiler_params=limit(8),
    )(w, s)


def load_kernel(place, a_ref, b_ref, o_ref):
    o_ref[...] = a_ref[0:8, 0:128] + b_ref[0:8, 0:128]


def load(place, a, b):
    return pl.pallas_call(
        load_kernel,
        out_shape=jax.ShapeDtypeStruct((8, 128), a.dtype),
        in_specs=[SM] + [VM] * 2,
        out_specs=VM,
        compiler_params=limit(16),
    )(place, a, b)


def matmul_kernel(pieces, count, place, ta_ref, tb_ref, *refs):
    shards, outs = refs[:count], refs[count + 1 : -2]
    w_ref, p_ref = refs[-2:]
    for at, (which, row) in enumerate(pieces):
        w_ref[at * 32 : at * 32 + 32] = shards[which][row : row + 32]
    here = place[0]

    def half(h, _):
        rows = pl.ds(pl.multiple_of(h * 512, 512), 512)
        for k, t_ref in enumerate((ta_ref, tb_ref)):
            p_ref[k, rows] = lax.dot_general(
                t_ref[rows], w_ref[...], NT, preferred_element_type=jnp.float32
            ).astype(jnp.bfloat16)
        return 0

    lax.fori_loop(0, 2, half, 0)
    split = len(outs) // 4
    for i, dx in enumerate(ORDER):
        for l in range(2):
            row = pl.multiple_of(place[1 + i] * 256 + (here ^ l) * 128, 128)
            for k in range(2):
                out = outs[dx * split + l * (split - 1)]
                to = l * 256 * (2 - split) + k * 128
                out[to : to + 128] = p_ref[k, pl.ds(row, 128)]


def matmul(place, ta, tb, tiles, arrays, ready, split):
    names, pieces = [], []
    for tile in tiles:
        for half in range(2):
            for name, row in tile:
                if name not in names:
                    names.append(name)
                pieces.append((names.index(name), row + half * 32))
    n, depth = 32 * len(pieces), ta.shape[1]
    return pl.pallas_call(
        functools.partial(matmul_kernel, pieces, len(names)),
        out_shape=[jax.ShapeDtypeStruct((512 // split, n), jnp.bfloat16)] * (4 * split),
        in_specs=[SM] + [VM] * (3 + len(names)),
        out_specs=[VM] * (4 * split),
        scratch_shapes=[
            pltpu.VMEM((n, depth), jnp.bfloat16),
            pltpu.VMEM((2, 1024, n), jnp.bfloat16),
        ],
        compiler_params=limit(24),
        cost_estimate=pl.CostEstimate(
            flops=2 * 2048 * n * depth,
            bytes_accessed=2 * (2048 * depth + n * depth + 2048 * n),
            transcendentals=0,
        ),
    )(place, ta, tb, *[arrays[k] for k in names], ready)


def combine_kernel(a_ref, b_ref, c_ref, d_ref, keep_ref, send_ref):
    f = lambda r, s: r[s].astype(jnp.float32)
    lo, hi = slice(0, 256), slice(256, 512)
    keep_ref[...] = (f(a_ref, lo) + f(b_ref, lo)) + (f(c_ref, lo) + f(d_ref, lo))
    send_ref[...] = ((f(a_ref, hi) + f(b_ref, hi)) + (f(c_ref, hi) + f(d_ref, hi))).astype(jnp.bfloat16)


def combine(parts):
    n = parts[0].shape[1]
    return pl.pallas_call(
        combine_kernel,
        out_shape=[jax.ShapeDtypeStruct((256, n), jnp.float32), jax.ShapeDtypeStruct((256, n), jnp.bfloat16)],
        in_specs=[VM] * 4,
        out_specs=[VM] * 2,
        compiler_params=limit(8),
    )(*parts)


def gated_kernel(sizes, *refs):
    parts, (mine_ref, other_ref) = refs[:-2], refs[-2:]
    for rows, o_ref in ((0, mine_ref), (128, other_ref)):

        def total(col):
            terms = [p[rows : rows + 128, col : col + 128].astype(jnp.float32) for p in parts]
            while len(terms) > 1:
                terms = [a + c for a, c in zip(terms[::2], terms[1::2])]
            return terms[0]

        col = 0
        for b, size in enumerate(sizes):
            gate = total(col)
            up = total(col + 128) if size == 4 else pltpu.roll(gate, 64, 1)
            col += 64 * size
            o_ref[:, b * 128 : b * 128 + 128] = gate / (1.0 + jnp.exp(-gate)) * up


def gated(parts, tiles):
    sizes = [len(tile) for tile in tiles]
    half = jax.ShapeDtypeStruct((128, len(sizes) * 128), jnp.float32)
    return pl.pallas_call(
        functools.partial(gated_kernel, sizes),
        out_shape=[half, half],
        in_specs=[VM] * len(parts),
        out_specs=[VM] * 2,
        compiler_params=limit(8),
    )(*parts)


def finish_kernel(place, docs, *refs):
    mine, theirs, o_ref = refs[:3], refs[3:6], refs[6]
    core, zh, y = place[5], place[6], place[7]
    live = -place[8]
    for i in range(docs.shape[1]):
        live += docs[0, i]
    rows = lax.broadcasted_iota(jnp.int32, (128, 128), 0)
    seg = lax.broadcasted_iota(jnp.int32, (128, 128), 1) // 32
    keep = rows < live
    first = jnp.full((128, 128), core, jnp.int32) == 0
    turn = lambda v, s: pltpu.roll(v, s % 128, 1) if s % 128 else v

    def ordered(side, ry):
        whole = None
        for rz in range(NZ):
            g, t, i = WHERE[(ry, rz)]
            piece = turn(side[g][:, t * 128 : t * 128 + 128], 32 * (rz - i))
            whole = piece if whole is None else jnp.where(seg == rz, piece, whole)
        return pltpu.roll(jnp.where(keep, whole, 0.0), zh * 32, 1)

    for ry in range(NY):
        m, t = ordered(mine, ry), ordered(theirs, ry)
        even, odd = jnp.where(first, m, t), jnp.where(first, t, m)
        lo = jnp.where(seg < 2, jnp.where(seg == 0, even, turn(odd, 32)), jnp.where(seg == 2, turn(even, 32), turn(odd, 64)))
        hi = jnp.where(seg < 2, jnp.where(seg == 0, turn(even, 64), turn(odd, 96)), jnp.where(seg == 2, turn(even, 96), odd))
        block = lax.rem(y + ry, NY) * 256
        o_ref[:, pl.ds(pl.multiple_of(block, 128), 128)] = lo
        o_ref[:, pl.ds(pl.multiple_of(block + 128, 128), 128)] = hi


def finish(place, docs, mine, theirs):
    return pl.pallas_call(
        finish_kernel,
        out_shape=jax.ShapeDtypeStruct((128, 1024), jnp.float32),
        in_specs=[SM] * 2 + [VM] * 6,
        out_specs=VM,
        compiler_params=limit(8),
    )(place, docs, *mine, *theirs)


def per_device(tokens, panel_weights, panel_scales, doc_lengths):
    seq, width = lax.axis_index("seq"), lax.axis_index("width")
    core, zh, y = seq & 1, (seq >> 1) & 3, seq >> 3
    x, zl = width >> 1, width & 1

    place = jnp.stack(
        [zl] + [(x + dx) & 3 for dx in ORDER] + [core, zh, y, width * 128]
    ).astype(jnp.int32)
    partner = seq_shift(tokens, flip=1)
    w = jnp.transpose(panel_weights, (0, 2, 1)).reshape(64, -1)
    s = jnp.transpose(panel_scales, (0, 2, 1)).reshape(64, -1)
    own = dequant(w, s)

    below, above = seq_shift(own, dz=1), seq_shift(own, dz=-1)
    own_p, own_m = seq_shift(own, dy=-1), seq_shift(own, dy=1)
    own_o = seq_shift(own, dy=2)
    ready = load(place, tokens, partner)
    far = seq_shift(own, dz=2)
    side = jnp.concatenate([below, above], 0)
    side_p, side_m = seq_shift(side, dy=-1), seq_shift(side, dy=1)
    far_o = seq_shift(own_o, dz=2)
    far_p, far_m = seq_shift(far, dy=-1), seq_shift(far, dy=1)
    below_o = seq_shift(side_m[:64], dy=1)
    above_o = seq_shift(side_p[64:], dy=-1)

    arrays = dict(
        own=own, own_p=own_p, own_m=own_m, own_o=own_o,
        side=side, side_p=side_p, side_m=side_m,
        far=far, far_p=far_p, far_m=far_m, far_o=far_o, below_o=below_o, above_o=above_o,
    )
    tag = {0: "", 1: "_p", 3: "_m", 2: "_o"}

    def shard(ry, rz):
        if rz == 0:
            return "own" + tag[ry], 0
        if rz == 2:
            return "far" + tag[ry], 0
        if ry == 2:
            return ("above_o" if rz == 1 else "below_o"), 0
        return "side" + tag[ry], (64 if rz == 1 else 0)

    mine, theirs = [], []
    for g, tiles in enumerate(GROUPS):
        named = [[shard(*s) for s in tile] for tile in tiles]
        outs = matmul(place, tokens, partner, named, arrays, ready, 1 if g < 2 else 2)
        if g < 2:
            got = [width_shift(outs[dx], dx, 0) for dx in (2, 1, 3)]
            keep, send = combine([outs[0]] + got)
            parts = [keep, width_shift(send, 0, 1)]
        else:
            parts = [outs[0]]
            for dx, dl in ((2, 1), (2, 0), (1, 1), (3, 1), (1, 0), (3, 0), (0, 1)):
                parts.append(width_shift(outs[dx * 2 + dl], dx, dl))
        a, b = gated(parts, tiles)
        mine.append(a)
        theirs.append(seq_shift(b, flip=1))
    return finish(place, doc_lengths, mine, theirs)


def solution(mesh):
    in_specs = (P("seq", "width"), P(None, "width", "seq"), P(None, "width", "seq"), P("seq", None))
    out_specs = P(("seq", "width"), None)
    return jax.shard_map(
        per_device, mesh=mesh, in_specs=in_specs, out_specs=out_specs, check_vma=False
    )
```

```python
import functools

import jax
import jax.numpy as jnp
from jax import lax
from jax.experimental import pallas as pl
from jax.experimental.pallas import tpu as pltpu
from jax.sharding import PartitionSpec as P


NY, NZ, NX = 4, 4, 4
ORDER = (2, 1, 3, 0)
NT = (((1,), (1,)), ((), ()))
GROUPS = (
    (((0, 0), (1, 0), (3, 0), (2, 0)), ((0, 1), (0, 3))),
    (((1, 1), (1, 3), (3, 1), (3, 3)),),
    (((0, 2), (1, 2), (3, 2), (2, 2)), ((2, 1), (2, 3))),
)


VM = pl.BlockSpec(memory_space=pltpu.VMEM)
SM = pl.BlockSpec(memory_space=pltpu.SMEM)


def limit(mib):
    return pltpu.CompilerParams(vmem_limit_bytes=mib << 20)


def seq_shift(v, dy=0, dz=0, flip=0):
    pairs = []
    for y in range(NY):
        for z in range(NZ):
            for c in range(2):
                to = (((y + dy) % NY) * NZ + (z + dz) % NZ) * 2 + (c ^ flip)
                pairs.append(((y * NZ + z) * 2 + c, to))
    return lax.ppermute(v, "seq", pairs)


def width_shift(v, dx, dl):
    pairs = []
    for x in range(NX):
        for l in range(2):
            pairs.append((x * 2 + l, ((x + dx) % NX) * 2 + (l ^ dl)))
    return lax.ppermute(v, "width", pairs)


def dequant_kernel(w_hbm, s_hbm, o_ref, w_ref, s_ref, sem):
    copies = [
        pltpu.make_async_copy(w_hbm, w_ref, sem.at[0]),
        pltpu.make_async_copy(s_hbm, s_ref, sem.at[1]),
    ]
    for copy in copies:
        copy.start()
    groups = s_ref.shape[1]
    depth = w_ref.shape[1]
    row = lax.broadcasted_iota(jnp.int32, (groups, depth), 0)
    col = lax.broadcasted_iota(jnp.int32, (groups, depth), 1)
    pick = jnp.where(col // 16 == row, 1.0, 0.0).astype(jnp.float32)
    copies[1].wait()
    spread = jnp.dot(
        s_ref[...], pick, precision=lax.Precision.HIGHEST,
        preferred_element_type=jnp.float32,
    )
    copies[0].wait()
    o_ref[...] = (w_ref[...].astype(jnp.float32) * spread).astype(jnp.bfloat16)


def dequant(w, s):
    return pl.pallas_call(
        dequant_kernel,
        out_shape=jax.ShapeDtypeStruct(w.shape, jnp.bfloat16),
        in_specs=[pl.BlockSpec(memory_space=pl.ANY)] * 2,
        out_specs=VM,
        scratch_shapes=[
            pltpu.VMEM(w.shape, w.dtype),
            pltpu.VMEM(s.shape, s.dtype),
            pltpu.SemaphoreType.DMA((2,)),
        ],
        compiler_params=limit(62),
    )(w, s)


def load_kernel(place, a_ref, b_ref, o_ref):
    o_ref[...] = a_ref[0:8, 0:128] + b_ref[0:8, 0:128]


def load(place, a, b):
    return pl.pallas_call(
        load_kernel,
        out_shape=jax.ShapeDtypeStruct((8, 128), a.dtype),
        in_specs=[SM] + [VM] * 2,
        out_specs=VM,
        compiler_params=limit(16),
    )(place, a, b)


def matmul_kernel(pieces, count, place, ta_ref, tb_ref, *refs):
    shards, outs = refs[:count], refs[count + 1 : -2]
    w_ref, p_ref = refs[-2:]
    for at, (which, row) in enumerate(pieces):
        w_ref[at * 32 : at * 32 + 32] = shards[which][row : row + 32]
    here = place[0]

    def half(h, _):
        rows = pl.ds(pl.multiple_of(h * 512, 512), 512)
        for k, t_ref in enumerate((ta_ref, tb_ref)):
            p_ref[k, rows] = lax.dot_general(
                t_ref[rows], w_ref[...], NT, preferred_element_type=jnp.float32
            ).astype(jnp.bfloat16)
        return 0

    lax.fori_loop(0, 2, half, 0)
    split = len(outs) // 4
    for i, dx in enumerate(ORDER):
        for l in range(2):
            row = pl.multiple_of(place[1 + i] * 256 + (here ^ l) * 128, 128)
            for k in range(2):
                out = outs[dx * split + l * (split - 1)]
                to = l * 256 * (2 - split) + k * 128
                out[to : to + 128] = p_ref[k, pl.ds(row, 128)]


def matmul(place, ta, tb, tiles, arrays, ready, split):
    names, pieces = [], []
    for tile in tiles:
        for half in range(2):
            for name, row in tile:
                if name not in names:
                    names.append(name)
                pieces.append((names.index(name), row + half * 32))
    n, depth = 32 * len(pieces), ta.shape[1]
    return pl.pallas_call(
        functools.partial(matmul_kernel, pieces, len(names)),
        out_shape=[jax.ShapeDtypeStruct((512 // split, n), jnp.bfloat16)] * (4 * split),
        in_specs=[SM] + [VM] * (3 + len(names)),
        out_specs=[VM] * (4 * split),
        scratch_shapes=[
            pltpu.VMEM((n, depth), jnp.bfloat16),
            pltpu.VMEM((2, 1024, n), jnp.bfloat16),
        ],
        compiler_params=limit(24),
        cost_estimate=pl.CostEstimate(
            flops=2 * 2048 * n * depth,
            bytes_accessed=2 * (2048 * depth + n * depth + 2048 * n),
            transcendentals=0,
        ),
    )(place, ta, tb, *[arrays[k] for k in names], ready)


def combine_kernel(a_ref, b_ref, c_ref, d_ref, keep_ref, send_ref):
    f = lambda r, s: r[s].astype(jnp.float32)
    lo, hi = slice(0, 256), slice(256, 512)
    keep_ref[...] = (f(a_ref, lo) + f(b_ref, lo)) + (f(c_ref, lo) + f(d_ref, lo))
    send_ref[...] = ((f(a_ref, hi) + f(b_ref, hi)) + (f(c_ref, hi) + f(d_ref, hi))).astype(jnp.bfloat16)


def combine(parts):
    n = parts[0].shape[1]
    return pl.pallas_call(
        combine_kernel,
        out_shape=[jax.ShapeDtypeStruct((256, n), jnp.float32), jax.ShapeDtypeStruct((256, n), jnp.bfloat16)],
        in_specs=[VM] * 4,
        out_specs=[VM] * 2,
        compiler_params=limit(8),
    )(*parts)


def gated_kernel(sizes, *refs):
    parts, (mine_ref, other_ref) = refs[:-2], refs[-2:]
    for rows, o_ref in ((0, mine_ref), (128, other_ref)):

        def total(col):
            terms = [p[rows : rows + 128, col : col + 128].astype(jnp.float32) for p in parts]
            while len(terms) > 1:
                terms = [a + c for a, c in zip(terms[::2], terms[1::2])]
            return terms[0]

        col = 0
        for b, size in enumerate(sizes):
            gate = total(col)
            up = total(col + 128) if size == 4 else pltpu.roll(gate, 64, 1)
            col += 64 * size
            o_ref[:, b * 128 : b * 128 + 128] = gate / (1.0 + jnp.exp(-gate)) * up


def gated(parts, tiles):
    sizes = [len(tile) for tile in tiles]
    half = jax.ShapeDtypeStruct((128, len(sizes) * 128), jnp.float32)
    return pl.pallas_call(
        functools.partial(gated_kernel, sizes),
        out_shape=[half, half],
        in_specs=[VM] * len(parts),
        out_specs=[VM] * 2,
        compiler_params=limit(8),
    )(*parts)


def place_kernel(groups, start, place, docs, *refs):
    count = len(groups)
    mine, theirs, o_ref = refs[:count], refs[count : 2 * count], refs[-1]
    core, zh, y = place[5], place[6], place[7]
    live = -place[8]
    for i in range(docs.shape[1]):
        live += docs[0, i]
    keep = lax.broadcasted_iota(jnp.int32, (128, 128), 0) < live
    lanes = lax.broadcasted_iota(jnp.int32, (128, 128), 1)
    o_ref[...] = jnp.zeros(o_ref.shape, o_ref.dtype) if start else refs[2 * count][...]
    for at, g in enumerate(groups):
        for side, c in ((mine, core), (theirs, 1 - core)):
            for t, tile in enumerate(GROUPS[g]):
                value = side[at][:, t * 128 : t * 128 + 128]
                for i, (ry, rz) in enumerate(tile):
                    z = (zh + rz) & 3
                    lane = (z & 1) * 64 + c * 32
                    moved = pltpu.roll(value, (lane + 128 - 32 * i) & 127, 1)
                    here = keep & (lanes >= lane) & (lanes < lane + 32)
                    block = ((y + ry) & 3) * 256 + (z >> 1) * 128
                    to = pl.ds(pl.multiple_of(block, 128), 128)
                    o_ref[:, to] = jnp.where(here, moved, o_ref[:, to])


def put(groups, place, docs, mine, theirs, base=None):
    args = [*mine, *theirs] + ([] if base is None else [base])
    return pl.pallas_call(
        functools.partial(place_kernel, groups, base is None),
        out_shape=jax.ShapeDtypeStruct((128, 1024), jnp.float32),
        in_specs=[SM] * 2 + [VM] * len(args),
        out_specs=VM,
        compiler_params=limit(8),
    )(place, docs, *args)


def per_device(tokens, panel_weights, panel_scales, doc_lengths):
    seq, width = lax.axis_index("seq"), lax.axis_index("width")
    core, zh, y = seq & 1, (seq >> 1) & 3, seq >> 3
    x, zl = width >> 1, width & 1

    place = jnp.stack(
        [zl] + [(x + dx) & 3 for dx in ORDER] + [core, zh, y, width * 128]
    ).astype(jnp.int32)
    partner = seq_shift(tokens, flip=1)
    w = jnp.transpose(panel_weights, (0, 2, 1)).reshape(64, -1)
    s = jnp.transpose(panel_scales, (0, 2, 1)).reshape(64, -1)
    own = dequant(w, s)

    below, above = seq_shift(own, dz=1), seq_shift(own, dz=-1)
    own_p, own_m = seq_shift(own, dy=-1), seq_shift(own, dy=1)
    own_o = seq_shift(own, dy=2)
    ready = load(place, tokens, partner)
    far = seq_shift(own, dz=2)
    side = jnp.concatenate([below, above], 0)
    side_p, side_m = seq_shift(side, dy=-1), seq_shift(side, dy=1)
    far_o = seq_shift(own_o, dz=2)
    far_p, far_m = seq_shift(far, dy=-1), seq_shift(far, dy=1)
    below_o = seq_shift(side_m[:64], dy=1)
    above_o = seq_shift(side_p[64:], dy=-1)

    arrays = dict(
        own=own, own_p=own_p, own_m=own_m, own_o=own_o,
        side=side, side_p=side_p, side_m=side_m,
        far=far, far_p=far_p, far_m=far_m, far_o=far_o, below_o=below_o, above_o=above_o,
    )
    tag = {0: "", 1: "_p", 3: "_m", 2: "_o"}

    def shard(ry, rz):
        if rz == 0:
            return "own" + tag[ry], 0
        if rz == 2:
            return "far" + tag[ry], 0
        if ry == 2:
            return ("above_o" if rz == 1 else "below_o"), 0
        return "side" + tag[ry], (64 if rz == 1 else 0)

    mine, theirs = [], []
    for g, tiles in enumerate(GROUPS):
        named = [[shard(*s) for s in tile] for tile in tiles]
        outs = matmul(place, tokens, partner, named, arrays, ready, 1 if g < 2 else 2)
        if g < 2:
            got = [width_shift(outs[dx], dx, 0) for dx in (2, 1, 3)]
            keep, send = combine([outs[0]] + got)
            parts = [keep, width_shift(send, 0, 1)]
        else:
            parts = [outs[0]]
            for dx, dl in ((2, 1), (2, 0), (1, 1), (3, 1), (1, 0), (3, 0), (0, 1)):
                parts.append(width_shift(outs[dx * 2 + dl], dx, dl))
        a, b = gated(parts, tiles)
        mine.append(a)
        theirs.append(seq_shift(b, flip=1))
    base = None
    for g in range(3):
        base = put((g,), place, doc_lengths, mine[g : g + 1], theirs[g : g + 1], base)
    return base


def solution(mesh):
    in_specs = (P("seq", "width"), P(None, "width", "seq"), P(None, "width", "seq"), P("seq", None))
    out_specs = P(("seq", "width"), None)
    return jax.shard_map(
        per_device, mesh=mesh, in_specs=in_specs, out_specs=out_specs, check_vma=False
    )
```

```python
import functools

import jax
import jax.numpy as jnp
from jax import lax
from jax.experimental import pallas as pl
from jax.experimental.pallas import tpu as pltpu
from jax.sharding import PartitionSpec as P


NY, NZ, NX = 4, 4, 4
ORDER = (2, 1, 3, 0)
NT = (((1,), (1,)), ((), ()))
GROUPS = (
    (((0, 0), (1, 0), (3, 0), (2, 0)), ((0, 1), (0, 3))),
    (((1, 1), (1, 3), (3, 1), (3, 3)),),
    (((0, 2), (1, 2), (3, 2), (2, 2)), ((2, 1), (2, 3))),
)


VM = pl.BlockSpec(memory_space=pltpu.VMEM)
SM = pl.BlockSpec(memory_space=pltpu.SMEM)


def limit(mib):
    return pltpu.CompilerParams(vmem_limit_bytes=mib << 20)


def seq_shift(v, dy=0, dz=0, flip=0):
    pairs = []
    for y in range(NY):
        for z in range(NZ):
            for c in range(2):
                to = (((y + dy) % NY) * NZ + (z + dz) % NZ) * 2 + (c ^ flip)
                pairs.append(((y * NZ + z) * 2 + c, to))
    return lax.ppermute(v, "seq", pairs)


def width_shift(v, dx, dl):
    pairs = []
    for x in range(NX):
        for l in range(2):
            pairs.append((x * 2 + l, ((x + dx) % NX) * 2 + (l ^ dl)))
    return lax.ppermute(v, "width", pairs)


def dequant_kernel(w_ref, s_ref, o_ref):
    groups = s_ref.shape[1]
    depth = w_ref.shape[1]
    row = lax.broadcasted_iota(jnp.int32, (groups, depth), 0)
    col = lax.broadcasted_iota(jnp.int32, (groups, depth), 1)
    pick = jnp.where(col // 16 == row, 1.0, 0.0).astype(jnp.float32)
    spread = jnp.dot(
        s_ref[...], pick, precision=lax.Precision.HIGHEST,
        preferred_element_type=jnp.float32,
    )
    o_ref[...] = (w_ref[...].astype(jnp.float32) * spread).astype(jnp.bfloat16)


def dequant(w, s):
    return pl.pallas_call(
        dequant_kernel,
        out_shape=jax.ShapeDtypeStruct(w.shape, jnp.bfloat16),
        in_specs=[VM, VM],
        out_specs=VM,
        compiler_params=limit(8),
    )(w, s)


def load_kernel(place, a_ref, b_ref, o_ref):
    o_ref[...] = a_ref[0:8, 0:128] + b_ref[0:8, 0:128]


def load(place, a, b):
    return pl.pallas_call(
        load_kernel,
        out_shape=jax.ShapeDtypeStruct((8, 128), a.dtype),
        in_specs=[SM] + [VM] * 2,
        out_specs=VM,
        compiler_params=limit(16),
    )(place, a, b)


def matmul_kernel(pieces, count, place, ta_ref, tb_ref, *refs):
    shards, outs = refs[:count], refs[count + 1 : -2]
    w_ref, p_ref = refs[-2:]
    for at, (which, row) in enumerate(pieces):
        w_ref[at * 32 : at * 32 + 32] = shards[which][row : row + 32]
    here = place[0]

    def half(h, _):
        rows = pl.ds(pl.multiple_of(h * 512, 512), 512)
        for k, t_ref in enumerate((ta_ref, tb_ref)):
            p_ref[k, rows] = lax.dot_general(
                t_ref[rows], w_ref[...], NT, preferred_element_type=jnp.float32
            ).astype(jnp.bfloat16)
        return 0

    lax.fori_loop(0, 2, half, 0)
    split = len(outs) // 4
    for i, dx in enumerate(ORDER):
        for l in range(2):
            row = pl.multiple_of(place[1 + i] * 256 + (here ^ l) * 128, 128)
            for k in range(2):
                out = outs[dx * split + l * (split - 1)]
                to = l * 256 * (2 - split) + k * 128
                out[to : to + 128] = p_ref[k, pl.ds(row, 128)]


def matmul(place, ta, tb, tiles, arrays, ready, split):
    names, pieces = [], []
    for tile in tiles:
        for half in range(2):
            for name, row in tile:
                if name not in names:
                    names.append(name)
                pieces.append((names.index(name), row + half * 32))
    n, depth = 32 * len(pieces), ta.shape[1]
    return pl.pallas_call(
        functools.partial(matmul_kernel, pieces, len(names)),
        out_shape=[jax.ShapeDtypeStruct((512 // split, n), jnp.bfloat16)] * (4 * split),
        in_specs=[SM] + [VM] * (3 + len(names)),
        out_specs=[VM] * (4 * split),
        scratch_shapes=[
            pltpu.VMEM((n, depth), jnp.bfloat16),
            pltpu.VMEM((2, 1024, n), jnp.bfloat16),
        ],
        compiler_params=limit(24),
        cost_estimate=pl.CostEstimate(
            flops=2 * 2048 * n * depth,
            bytes_accessed=2 * (2048 * depth + n * depth + 2048 * n),
            transcendentals=0,
        ),
    )(place, ta, tb, *[arrays[k] for k in names], ready)


def combine_kernel(a_ref, b_ref, c_ref, d_ref, keep_ref, send_ref):
    f = lambda r, s: r[s].astype(jnp.float32)
    lo, hi = slice(0, 256), slice(256, 512)
    keep_ref[...] = (f(a_ref, lo) + f(b_ref, lo)) + (f(c_ref, lo) + f(d_ref, lo))
    send_ref[...] = ((f(a_ref, hi) + f(b_ref, hi)) + (f(c_ref, hi) + f(d_ref, hi))).astype(jnp.bfloat16)


def combine(parts):
    n = parts[0].shape[1]
    return pl.pallas_call(
        combine_kernel,
        out_shape=[jax.ShapeDtypeStruct((256, n), jnp.float32), jax.ShapeDtypeStruct((256, n), jnp.bfloat16)],
        in_specs=[VM] * 4,
        out_specs=[VM] * 2,
        compiler_params=limit(8),
    )(*parts)


def gated_kernel(sizes, *refs):
    parts, (mine_ref, other_ref) = refs[:-2], refs[-2:]
    for rows, o_ref in ((0, mine_ref), (128, other_ref)):

        def total(col):
            terms = [p[rows : rows + 128, col : col + 128].astype(jnp.float32) for p in parts]
            while len(terms) > 1:
                terms = [a + c for a, c in zip(terms[::2], terms[1::2])]
            return terms[0]

        col = 0
        for b, size in enumerate(sizes):
            gate = total(col)
            up = total(col + 128) if size == 4 else pltpu.roll(gate, 64, 1)
            col += 64 * size
            o_ref[:, b * 128 : b * 128 + 128] = gate / (1.0 + jnp.exp(-gate)) * up


def gated(parts, tiles):
    sizes = [len(tile) for tile in tiles]
    half = jax.ShapeDtypeStruct((128, len(sizes) * 128), jnp.float32)
    return pl.pallas_call(
        functools.partial(gated_kernel, sizes),
        out_shape=[half, half],
        in_specs=[VM] * len(parts),
        out_specs=[VM] * 2,
        compiler_params=limit(8),
    )(*parts)


def place_kernel(groups, start, place, docs, *refs):
    count = len(groups)
    mine, theirs, o_ref = refs[:count], refs[count : 2 * count], refs[-1]
    core, zh, y = place[5], place[6], place[7]
    live = -place[8]
    for i in range(docs.shape[1]):
        live += docs[0, i]
    keep = lax.broadcasted_iota(jnp.int32, (128, 128), 0) < live
    lanes = lax.broadcasted_iota(jnp.int32, (128, 128), 1)
    o_ref[...] = jnp.zeros(o_ref.shape, o_ref.dtype) if start else refs[2 * count][...]
    for at, g in enumerate(groups):
        for side, c in ((mine, core), (theirs, 1 - core)):
            for t, tile in enumerate(GROUPS[g]):
                value = side[at][:, t * 128 : t * 128 + 128]
                for i, (ry, rz) in enumerate(tile):
                    z = (zh + rz) & 3
                    lane = (z & 1) * 64 + c * 32
                    moved = pltpu.roll(value, (lane + 128 - 32 * i) & 127, 1)
                    here = keep & (lanes >= lane) & (lanes < lane + 32)
                    block = ((y + ry) & 3) * 256 + (z >> 1) * 128
                    to = pl.ds(pl.multiple_of(block, 128), 128)
                    o_ref[:, to] = jnp.where(here, moved, o_ref[:, to])


def put(groups, place, docs, mine, theirs, base=None):
    args = [*mine, *theirs] + ([] if base is None else [base])
    return pl.pallas_call(
        functools.partial(place_kernel, groups, base is None),
        out_shape=jax.ShapeDtypeStruct((128, 1024), jnp.float32),
        in_specs=[SM] * 2 + [VM] * len(args),
        out_specs=VM,
        compiler_params=limit(8),
    )(place, docs, *args)


def per_device(tokens, panel_weights, panel_scales, doc_lengths):
    seq, width = lax.axis_index("seq"), lax.axis_index("width")
    core, zh, y = seq & 1, (seq >> 1) & 3, seq >> 3
    x, zl = width >> 1, width & 1

    place = jnp.stack(
        [zl] + [(x + dx) & 3 for dx in ORDER] + [core, zh, y, width * 128]
    ).astype(jnp.int32)
    partner = seq_shift(tokens, flip=1)
    w = jnp.transpose(panel_weights, (0, 2, 1)).reshape(64, -1)
    s = jnp.transpose(panel_scales, (0, 2, 1)).reshape(64, -1)
    own = dequant(w, s)

    below, above = seq_shift(own, dz=1), seq_shift(own, dz=-1)
    own_p, own_m = seq_shift(own, dy=-1), seq_shift(own, dy=1)
    own_o = seq_shift(own, dy=2)
    ready = load(place, tokens, partner)
    far = seq_shift(own, dz=2)
    side = jnp.concatenate([below, above], 0)
    side_p, side_m = seq_shift(side, dy=-1), seq_shift(side, dy=1)
    far_o = seq_shift(own_o, dz=2)
    far_p, far_m = seq_shift(far, dy=-1), seq_shift(far, dy=1)
    below_o = seq_shift(side_m[:64], dy=1)
    above_o = seq_shift(side_p[64:], dy=-1)

    arrays = dict(
        own=own, own_p=own_p, own_m=own_m, own_o=own_o,
        side=side, side_p=side_p, side_m=side_m,
        far=far, far_p=far_p, far_m=far_m, far_o=far_o, below_o=below_o, above_o=above_o,
    )
    tag = {0: "", 1: "_p", 3: "_m", 2: "_o"}

    def shard(ry, rz):
        if rz == 0:
            return "own" + tag[ry], 0
        if rz == 2:
            return "far" + tag[ry], 0
        if ry == 2:
            return ("above_o" if rz == 1 else "below_o"), 0
        return "side" + tag[ry], (64 if rz == 1 else 0)

    mine, theirs = [], []
    for g, tiles in enumerate(GROUPS):
        named = [[shard(*s) for s in tile] for tile in tiles]
        outs = matmul(place, tokens, partner, named, arrays, ready, 1 if g < 2 else 2)
        if g < 2:
            got = [width_shift(outs[dx], dx, 0) for dx in (2, 1, 3)]
            keep, send = combine([outs[0]] + got)
            parts = [keep, width_shift(send, 0, 1)]
        else:
            parts = [outs[0]]
            for dx, dl in ((2, 1), (2, 0), (1, 1), (3, 1), (1, 0), (3, 0), (0, 1)):
                parts.append(width_shift(outs[dx * 2 + dl], dx, dl))
        a, b = gated(parts, tiles)
        mine.append(a)
        theirs.append(seq_shift(b, flip=1))
    base = None
    for g in range(3):
        base = put((g,), place, doc_lengths, mine[g : g + 1], theirs[g : g + 1], base)
    return base


def solution(mesh):
    in_specs = (P("seq", "width"), P(None, "width", "seq"), P(None, "width", "seq"), P("seq", None))
    out_specs = P(("seq", "width"), None)
    return jax.shard_map(
        per_device, mesh=mesh, in_specs=in_specs, out_specs=out_specs, check_vma=False
    )
```
